256 devices in a mesh: tm: 8 (over y, z_lo), chan: 32 (over z_hi, x, core).
Axes of the slice: x: 4, y: 4, z: 8 (z_hi: 4, z_lo: 2; z = z_hi * 2 + z_lo), core: 2. Of those that a mesh axis runs over, the one named last changes fastest.
Arguments:
- record: bfloat16 [8192, 32768], P('chan', 'tm'), may hold values from -6 to 6
- fan_mask: int32 [256, 8192], P('chan'), may hold values 0 or 1
Outputs:
- filtered: float32 [8192, 32768], P('chan', 'tm')
The draws below stay inside these ranges and needn't reach their ends.
All inputs are finite; a program needn't handle non-finite values. No bound on the sum of `fan_mask` on one device may be relied on, other than what follows from the above.
Results may differ from the reference program's by a relative error of at most 0.0084.
Values may be sent and summed in bfloat16 or wider, within the bound.
No kernel may reach another device: no remote copies, remote signals or barrier semaphores. Data moves between devices by JAX's collectives and lax.ppermute only.
A program may use at most 128 MiB of HBM per device.

```python
import math
import jax
import jax.numpy as jnp
from jax import lax

NCH = 8192
SECTION_A = 64
WIN = 512
SECTION_B = 128
HOP = 256
BINS = 256
FRAMES = 128
SAMPLES = 32768


def place_ends(entries, own_key, smallest, high):
    dims = entries.shape
    spot = [jax.random.randint(jax.random.fold_in(own_key, axis), (), 0, dims[axis]) for axis in range(len(dims))]
    entries = entries.at[tuple(spot)].set(smallest)
    longest = dims.index(max(dims))
    spot[longest] = (spot[longest] + 1) % dims[longest]
    return entries.at[tuple(spot)].set(high)


def levels(own_key, dims, split, low, top_value):
    loudness = 1.0
    for axis_at, shards_of in split:
        draws = jax.random.uniform(jax.random.fold_in(jax.random.fold_in(own_key, 6), axis_at), (shards_of,), jnp.float32, low / len(split), top_value / len(split))
        loudness = loudness * jnp.repeat(jnp.exp(draws), dims[axis_at] // shards_of).reshape((-1,) + (1,) * (len(dims) - 1 - axis_at))
    return loudness


def gaussian(own_key, dims, width, most, split=(), kind=jnp.bfloat16):
    entries = jax.random.normal(own_key, dims, jnp.float32) * width
    if len(split) > 0:
        entries = levels(own_key, dims, split, -0.22, 0.18) * entries
    return jnp.clip(entries, min=-most, max=most).astype(kind)


def setup_inputs(seed: int = 0) -> dict:
    key_list = jax.random.split(jax.random.key(seed), 3)
    record = gaussian(key_list[0], (NCH, SAMPLES), 1.0, 6.0, ((0, 32), (1, 8)))
    fan_mask = place_ends((jax.random.randint(key_list[1], (BINS, NCH), 0, 2) < 1).astype(jnp.int32), jax.random.fold_in(key_list[1], 1), 0, 1)
    return {"record": record, "fan_mask": fan_mask}


def hann_taper(length):
    steps = jnp.arange(length, dtype=jnp.int32).astype(jnp.float32)
    return 0.5 - 0.5 * jnp.cos(steps * (2.0 * math.pi / length))


def time_table(length, bins):
    rows = jnp.arange(length, dtype=jnp.int32)[:, None]
    cols = jnp.arange(bins, dtype=jnp.int32)[None, :]
    phase = ((rows * cols) % length).astype(jnp.float32) * (2.0 * math.pi / length)
    return jnp.concatenate([jnp.cos(phase), -jnp.sin(phase)], axis=1).astype(jnp.bfloat16)


def inverse_time_table(length, bins):
    rows = jnp.arange(bins, dtype=jnp.int32)[:, None]
    cols = jnp.arange(length, dtype=jnp.int32)[None, :]
    phase = ((rows * cols) % length).astype(jnp.float32) * (2.0 * math.pi / length)
    weight = jnp.where(rows == 0, 1.0, 2.0).astype(jnp.float32) / length
    return jnp.stack([weight * jnp.cos(phase), -weight * jnp.sin(phase)]).astype(jnp.bfloat16)


def block_table(order_len, exponent_sign):
    rows = jnp.arange(order_len, dtype=jnp.int32)[:, None]
    cols = jnp.arange(order_len, dtype=jnp.int32)[None, :]
    phase = ((rows * cols) % order_len).astype(jnp.float32) * (2.0 * math.pi / order_len)
    cosine = jnp.cos(phase)
    sine = exponent_sign * jnp.sin(phase)
    real_row = jnp.stack([cosine, sine], axis=1)
    imag_row = jnp.stack([-sine, cosine], axis=1)
    return jnp.stack([real_row, imag_row], axis=0).astype(jnp.bfloat16)


def twiddle_pair(row_count, col_count, total, exponent_sign):
    rows = jnp.arange(row_count, dtype=jnp.int32)[:, None]
    cols = jnp.arange(col_count, dtype=jnp.int32)[None, :]
    phase = ((rows * cols) % total).astype(jnp.float32) * (2.0 * math.pi / total)
    return jnp.cos(phase), exponent_sign * jnp.sin(phase)


def rotate(values, cosine, sine):
    return jnp.stack([values[0] * cosine - values[1] * sine, values[0] * sine + values[1] * cosine])


def wide_einsum(form, left, right):
    return jnp.einsum(form, left.astype(jnp.float32), right.astype(jnp.float32), precision=lax.Precision.HIGHEST)


def reference(record, fan_mask):
    taper = hann_taper(WIN)
    forward_time = time_table(WIN, BINS)
    inverse_time = inverse_time_table(WIN, BINS)
    outer_fwd = block_table(SECTION_A, -1.0)
    inner_fwd = block_table(SECTION_B, -1.0)
    inner_inv = block_table(SECTION_B, 1.0)
    outer_inv = block_table(SECTION_A, 1.0)
    fwd_cos, fwd_sin = twiddle_pair(SECTION_A, SECTION_B, NCH, -1.0)
    inv_cos, inv_sin = twiddle_pair(SECTION_A, SECTION_B, NCH, 1.0)
    fk_gate = fan_mask.reshape(BINS, SECTION_B, SECTION_A).transpose(0, 2, 1).astype(jnp.float32)
    padded = jnp.concatenate([record, jnp.zeros((NCH, HOP), record.dtype)], axis=1)

    def advance(previous, frame_index):
        frame_rows = lax.dynamic_slice_in_dim(padded, frame_index * HOP, WIN, 1)
        windowed = (frame_rows.astype(jnp.float32) * taper).astype(jnp.bfloat16)
        spectra = jnp.dot(windowed, forward_time, preferred_element_type=jnp.float32).astype(jnp.bfloat16)
        spectra = spectra.reshape(NCH, 2, BINS).transpose(1, 2, 0).reshape(2, BINS, SECTION_A, SECTION_B)
        section_one = wide_einsum('ikpq,ipoj->okjq', spectra, outer_fwd)
        section_one = rotate(section_one, fwd_cos, fwd_sin).astype(jnp.bfloat16)
        fk_plane = wide_einsum('ikjq,iqor->okjr', section_one, inner_fwd)
        fk_plane = (fk_plane * fk_gate[None]).astype(jnp.bfloat16)
        section_three = wide_einsum('ikjr,iroq->okjq', fk_plane, inner_inv)
        section_three = rotate(section_three, inv_cos, inv_sin).astype(jnp.bfloat16)
        restored = wide_einsum('ikjq,ijop->okpq', section_three, outer_inv) * (1.0 / NCH)
        restored = restored.astype(jnp.bfloat16).reshape(2, BINS, NCH)
        signal = wide_einsum('ikc,ikn->cn', restored, inverse_time)
        return signal[:, HOP:], signal[:, :HOP] + previous

    start = jnp.zeros((NCH, HOP), jnp.float32)
    _, output_blocks = lax.scan(advance, start, jnp.arange(FRAMES, dtype=jnp.int32))
    return output_blocks.transpose(1, 0, 2).reshape(NCH, SAMPLES)
```

```python
import functools

import jax
import jax.numpy as jnp
import numpy as np
from jax import lax
from jax.experimental import pallas as pl
from jax.experimental.pallas import tpu as pltpu
from jax.sharding import PartitionSpec as P

NCH = 8192
WIN = 512
HOP = 256
SLICE = 4
CHUNKS = 2
FR = SLICE // CHUNKS
BF = jnp.bfloat16
F32 = jnp.float32

ROUTES = [(0, 0), (2, 0), (2, 1), (1, 0), (1, 1), (3, 0), (3, 1), (0, 1)]
SHIFTS = (2, 1, 3)


def bf16_table(values):
    return jnp.asarray(values.astype(np.float32)).astype(BF)


def make_tables():
    n = np.arange(WIN)
    w, zb, ri, b = np.meshgrid(np.arange(8), np.arange(4), np.arange(2), np.arange(8), indexing="ij")
    k = (64 * zb + 8 * w + b).reshape(8, 64, 1)
    imag = ri.reshape(8, 64, 1) == 1
    phase = ((k * n) % WIN) * (2.0 * np.pi / WIN)
    wave = np.where(imag, -np.sin(phase), np.cos(phase))
    taper = 0.5 - 0.5 * np.cos(n * (2.0 * np.pi / WIN))
    forward = wave * taper
    inverse = wave * np.where(k == 0, 1.0, 2.0) / (WIN * NCH)
    e = np.arange(256)
    turn = (np.outer(e, e) % 256) * (2.0 * np.pi / 256)
    dft = np.concatenate([np.cos(turn), -np.sin(turn)], axis=1)
    idft = np.concatenate([np.cos(turn), np.sin(turn)], axis=1)
    twist = np.outer(np.arange(32), e) * (2.0 * np.pi / NCH)
    return (
        forward.astype(jnp.bfloat16),
        inverse.reshape(512, WIN).astype(jnp.bfloat16),
        dft.astype(jnp.bfloat16),
        idft.astype(jnp.bfloat16),
        np.cos(twist).astype(np.float32),
        np.sin(twist).astype(np.float32),
    )


def position():
    d = lax.axis_index("chan")
    z = lax.div(d, 8)
    x = lax.rem(lax.div(d, 2), 4)
    k = lax.rem(d, 2)
    return z, x, k


def route_to(x, k, dx, dc):
    return 2 * lax.rem(x + dx, 4) + (k if dc == 0 else 1 - k)


def route_from(x, k, dx, dc):
    return 2 * lax.rem(x + 4 - dx, 4) + (k if dc == 0 else 1 - k)


def z_permute(value, shift):
    pairs = [(8 * z + w, 8 * ((z + shift) % 4) + w) for z in range(4) for w in range(8)]
    return lax.ppermute(value, "chan", pairs)


def x_permute(value, dx, dc):
    pairs = [
        (8 * z + 2 * x + k, 8 * z + 2 * ((x + dx) % 4) + (k ^ dc))
        for z in range(4)
        for x in range(4)
        for k in range(2)
    ]
    return lax.ppermute(value, "chan", pairs)


def time_permute(value, by):
    peers = lax.axis_size("tm")
    return lax.ppermute(value, "tm", [(i, i + by) for i in range(peers) if 0 <= i + by < peers])


def cadd(a, b):
    return a[0] + b[0], a[1] + b[1]


def csub(a, b):
    return a[0] - b[0], a[1] - b[1]


def cturn(a, sign):
    return (-a[1], a[0]) if sign > 0 else (a[1], -a[0])


def cphase(a, num, den, sign):
    num = num % den
    if num == 0:
        return a
    if 4 * num == den:
        return cturn(a, sign)
    if 2 * num == den:
        return -a[0], -a[1]
    if 4 * num == 3 * den:
        return cturn(a, -sign)
    if 8 * num == den:
        h = np.float32(np.sqrt(0.5))
        t = cturn(a, sign)
        return (a[0] + t[0]) * h, (a[1] + t[1]) * h
    if 8 * num == 3 * den:
        h = np.float32(np.sqrt(0.5))
        t = cturn(a, sign)
        return (t[0] - a[0]) * h, (t[1] - a[1]) * h
    c = np.float32(np.cos(2 * np.pi * num / den))
    s = np.float32(sign * np.sin(2 * np.pi * num / den))
    return a[0] * c - a[1] * s, a[0] * s + a[1] * c


def dft4(v, sign):
    p, q = cadd(v[0], v[2]), csub(v[0], v[2])
    r, t = cadd(v[1], v[3]), cturn(csub(v[1], v[3]), sign)
    return [cadd(p, r), cadd(q, t), csub(p, r), csub(q, t)]


def dft8(v, sign):
    even = dft4(v[0::2], sign)
    odd = [cphase(a, i, 8, sign) for i, a in enumerate(dft4(v[1::2], sign))]
    return [cadd(a, b) for a, b in zip(even, odd)] + [csub(a, b) for a, b in zip(even, odd)]


def split_tile(tile):
    wide = tile.astype(F32)
    return wide[:8], wide[8:]


def join_tile(pair):
    return jnp.concatenate(pair, axis=0).astype(BF)


def stft_kernel(first, *refs):
    pieces, refs = refs[:4], refs[4:]
    if not first:
        edges, refs = refs[:4], refs[4:]
    table, refs = refs[0], refs[1:]
    outs, ordered = refs[:8], refs[8]
    z, x, k = position()
    for i, (dx, dc) in enumerate(ROUTES):
        ordered[64 * i : 64 * (i + 1), :] = table[route_to(x, k, dx, dc)]
    nt = (((1,), (1,)), ((), ()))
    for s in range(4):
        place = pl.ds(pl.multiple_of(lax.rem(z + 4 - s, 4) * 256, 256), 256)
        for f in range(FR):
            if first:
                got = lax.dot_general(
                    ordered[...], pieces[s][:, HOP * f : HOP * f + WIN], nt, preferred_element_type=F32
                )
            elif f == 0:
                got = lax.dot_general(
                    ordered[:, :HOP], edges[s][...], nt, preferred_element_type=F32
                ) + lax.dot_general(
                    ordered[:, HOP:], pieces[s][:, :HOP], nt, preferred_element_type=F32
                )
            else:
                got = lax.dot_general(
                    ordered[...],
                    pieces[s][:, HOP * (f - 1) : HOP * (f + 1)],
                    nt,
                    preferred_element_type=F32,
                )
            got = got.astype(BF)
            for i in range(8):
                outs[i][f, :, place] = got[64 * i : 64 * (i + 1)]


def stft(pieces, edges, table):
    first = edges is None
    whole = lambda a: pl.BlockSpec(a.shape, lambda i: (0,) * a.ndim)
    specs = [whole(a) for a in pieces]
    if not first:
        last = edges[0].shape[1] // HOP - 1
        specs += [pl.BlockSpec((256, HOP), lambda i: (0, last)) for _ in edges]
    specs.append(whole(table))
    shape = jax.ShapeDtypeStruct((FR, 64, 1024), BF)
    return pl.pallas_call(
        functools.partial(stft_kernel, first),
        grid=(1,),
        out_shape=[shape] * 8,
        in_specs=specs,
        out_specs=[pl.BlockSpec(shape.shape, lambda i: (0, 0, 0))] * 8,
        scratch_shapes=[pltpu.VMEM((512, WIN), BF)],
        cost_estimate=pl.CostEstimate(
            flops=2 * 512 * 512 * 1024 * FR, bytes_accessed=8 << 20, transcendentals=0
        ),
        name="stft",
    )(*pieces, *([] if first else edges), table)


def plane_kernel(*refs):
    pieces, masks, refs = refs[:8], refs[8:12], refs[12:]
    dft, idft, cosine, sine = refs[:4]
    outs, refs = refs[4:12], refs[12:]
    grid, mixed, gate, sems = refs
    rows = FR * 64
    z, x, k = position()
    copies = [
        pltpu.make_async_copy(pieces[i], grid.at[route_from(x, k, dx, dc)], sems.at[i])
        for i, (dx, dc) in enumerate(ROUTES)
    ]
    copies += [
        pltpu.make_async_copy(masks[s], gate.at[lax.rem(z + 4 - s, 4)], sems.at[8 + s])
        for s in range(4)
    ]
    for copy in copies:
        copy.start()
    for copy in copies:
        copy.wait()

    def forward(step, _):
        f = lax.div(step, 8)
        part = lax.rem(lax.div(step, 2), 4)
        lanes = pl.multiple_of(lax.rem(step, 2) * 128, 128)
        row = pl.ds(pl.multiple_of(part * 16, 16), 16)
        cut = pl.ds(pl.multiple_of(f * 64 + part * 16, 16), 16)

        def get(zz, w):
            return split_tile(grid[w, f, row, pl.ds(zz * 256 + lanes, 128)])

        for low in range(2):
            one, two = [], []
            for w in range(8):
                v = [get(zz, w) for zz in range(4)]
                if low == 0:
                    p, q = cadd(v[0], v[2]), cadd(v[1], v[3])
                else:
                    p, q = csub(v[0], v[2]), cturn(csub(v[1], v[3]), -1)
                one.append(cphase(cadd(p, q), w * low, 32, -1))
                two.append(cphase(csub(p, q), w * (low + 2), 32, -1))
            for j4, line in ((low, one), (low + 2, two)):
                for j8, (re, im) in enumerate(dft8(line, -1)):
                    m0 = j4 + 4 * j8
                    c = cosine[m0 : m0 + 1, pl.ds(lanes, 128)]
                    s = sine[m0 : m0 + 1, pl.ds(lanes, 128)]
                    mixed[m0, cut, pl.ds(lanes, 128)] = join_tile((re * c + im * s, im * c - re * s))
        return 0

    lax.fori_loop(0, FR * 8, forward, 0)

    def filter_rows(m0, _):
        spread = jnp.dot(mixed[m0], dft[...], preferred_element_type=F32)
        spread = spread.reshape(FR * 4, 2, 8, 512)
        re = spread[:, 0, :, :256] - spread[:, 1, :, 256:]
        im = spread[:, 0, :, 256:] + spread[:, 1, :, :256]
        keep = gate[:, m0].astype(F32)
        keep = jnp.concatenate([keep] * FR, axis=0)
        plane = jnp.stack([re * keep, im * keep], axis=1).reshape(rows, 256).astype(BF)
        spread = jnp.dot(plane, idft[...], preferred_element_type=F32)
        spread = spread.reshape(FR * 4, 2, 8, 512)
        re = spread[:, 0, :, :256] - spread[:, 1, :, 256:]
        im = spread[:, 0, :, 256:] + spread[:, 1, :, :256]
        c = cosine[pl.ds(m0, 1), :]
        s = sine[pl.ds(m0, 1), :]
        mixed[m0] = (
            jnp.stack([re * c - im * s, re * s + im * c], axis=1).reshape(rows, 256).astype(BF)
        )
        return 0

    lax.fori_loop(0, 32, filter_rows, 0)

    def backward(step, _):
        f = lax.div(step, 8)
        part = lax.rem(lax.div(step, 2), 4)
        lanes = pl.multiple_of(lax.rem(step, 2) * 128, 128)
        row = pl.ds(pl.multiple_of(part * 16, 16), 16)
        cut = pl.ds(pl.multiple_of(f * 64 + part * 16, 16), 16)
        for odd in range(2):
            lines = []
            for j4 in range(4):
                v = [split_tile(mixed[j4 + 4 * j8, cut, pl.ds(lanes, 128)]) for j8 in range(8)]
                if odd == 0:
                    u = [cadd(v[i], v[i + 4]) for i in range(4)]
                else:
                    u = [cphase(csub(v[i], v[i + 4]), i, 8, 1) for i in range(4)]
                lines.append(
                    [cphase(a, (2 * i + odd) * j4, 32, 1) for i, a in enumerate(dft4(u, 1))]
                )
            for i in range(4):
                for zz, pair in enumerate(dft4([lines[j4][i] for j4 in range(4)], 1)):
                    grid[2 * i + odd, f, row, pl.ds(zz * 256 + lanes, 128)] = join_tile(pair)
        return 0

    lax.fori_loop(0, FR * 8, backward, 0)
    copies = [
        pltpu.make_async_copy(grid.at[route_to(x, k, dx, dc)], outs[i], sems.at[i])
        for i, (dx, dc) in enumerate(ROUTES)
    ]
    for copy in copies:
        copy.start()
    for copy in copies:
        copy.wait()


def plane(pieces, masks, dft, idft, cosine, sine):
    whole = lambda a: pl.BlockSpec(a.shape, lambda: (0,) * a.ndim)
    anywhere = pl.BlockSpec(memory_space=pl.ANY)
    shape = jax.ShapeDtypeStruct((FR, 64, 1024), BF)
    return pl.pallas_call(
        plane_kernel,
        out_shape=[shape] * 8,
        in_specs=[anywhere] * 12 + [whole(a) for a in (dft, idft, cosine, sine)],
        out_specs=[anywhere] * 8,
        scratch_shapes=[
            pltpu.VMEM((8, FR, 64, 1024), BF),
            pltpu.VMEM((32, FR * 64, 256), BF),
            pltpu.VMEM((4, 32, 8, 256), BF),
            pltpu.SemaphoreType.DMA((12,)),
        ],
        cost_estimate=pl.CostEstimate(
            flops=4 * 32 * FR * 64 * 256 * 512 * 2, bytes_accessed=16 << 20, transcendentals=0
        ),
        name="plane",
    )(*pieces, *masks, dft, idft, cosine, sine)


def istft_kernel(first, last, *refs):
    pieces, refs = refs[:8], refs[8:]
    table, refs = refs[0], refs[1:]
    if not first:
        carried, refs = refs[0], refs[1:]
    outs, refs = refs[:4], refs[4:]
    if not last:
        carry, refs = refs[0], refs[1:]
    grid, sems = refs
    z, x, k = position()
    copies = [
        pltpu.make_async_copy(pieces[i], grid.at[:, route_from(x, k, dx, dc)], sems.at[i])
        for i, (dx, dc) in enumerate(ROUTES)
    ]
    for copy in copies:
        copy.start()
    for copy in copies:
        copy.wait()
    tn = (((0,), (0,)), ((), ()))
    for s in range(4):
        place = pl.ds(pl.multiple_of(lax.rem(z + s, 4) * 256, 256), 256)
        tail = None if first else carried[s]
        for f in range(FR):
            bins = grid[f, :, :, place].reshape(512, 256)
            signal = lax.dot_general(bins, table[...], tn, preferred_element_type=F32)
            head = signal[:, :HOP]
            if tail is not None:
                head = head + tail
            outs[s][:, HOP * f : HOP * (f + 1)] = head.astype(BF)
            tail = signal[:, HOP:]
        if last:
            outs[s][:, HOP * FR :] = tail.astype(BF)
        else:
            carry[s] = tail


def istft(pieces, table, carried, last):
    first = carried is None
    whole = lambda a: pl.BlockSpec(a.shape, lambda: (0,) * len(a.shape))
    anywhere = pl.BlockSpec(memory_space=pl.ANY)
    operands = [*pieces, table] + ([] if first else [carried])
    shapes = [jax.ShapeDtypeStruct((256, HOP * (FR + (1 if last else 0))), BF)] * 4
    if not last:
        shapes.append(jax.ShapeDtypeStruct((4, 256, HOP), F32))
    return pl.pallas_call(
        functools.partial(istft_kernel, first, last),
        out_shape=shapes,
        in_specs=[anywhere] * 8 + [whole(a) for a in operands[8:]],
        out_specs=[whole(a) for a in shapes],
        scratch_shapes=[pltpu.VMEM((FR, 8, 64, 1024), BF), pltpu.SemaphoreType.DMA((8,))],
        cost_estimate=pl.CostEstimate(
            flops=2 * 512 * 512 * 1024 * FR, bytes_accessed=8 << 20, transcendentals=0
        ),
        name="istft",
    )(*operands)


def join_kernel(*refs):
    pieces, edge, out = refs[: 4 * CHUNKS], refs[4 * CHUNKS], refs[4 * CHUNKS + 1]
    z, _, _ = position()
    for s in range(4):
        source = lax.rem(z + 4 - s, 4)
        start = pl.multiple_of(source * (SLICE * HOP), SLICE * HOP)
        ahead = pieces[4 * (CHUNKS - 1) + (s + 1) % 4][:, HOP * FR :].astype(F32)
        ahead = jnp.where(source == 0, edge[...].astype(F32), ahead)
        for i in range(CHUNKS):
            block = pieces[4 * i + s][:, : HOP * FR].astype(F32)
            if i == 0:
                out[:, pl.ds(start, HOP)] = block[:, :HOP] + ahead
                if FR > 1:
                    out[:, pl.ds(start + HOP, HOP * (FR - 1))] = block[:, HOP:]
            else:
                out[:, pl.ds(start + HOP * FR * i, HOP * FR)] = block


def join(chunks, edge, span):
    pieces = [a for chunk in chunks for a in chunk]
    rows = 64
    return pl.pallas_call(
        join_kernel,
        grid=(256 // rows,),
        out_shape=jax.ShapeDtypeStruct((256, span), F32),
        in_specs=[pl.BlockSpec((rows, a.shape[1]), lambda i: (i, 0)) for a in pieces]
        + [pl.BlockSpec((rows, HOP), lambda i: (i, 0))],
        out_specs=pl.BlockSpec((rows, span), lambda i: (i, 0)),
        cost_estimate=pl.CostEstimate(flops=1 << 20, bytes_accessed=8 << 20, transcendentals=0),
        name="join",
    )(*pieces, edge)


def body(record, fan_mask):
    channels, span = record.shape
    forward, inverse, dft, idft, cosine, sine = make_tables()
    forward, inverse, dft, idft = (jnp.asarray(a) for a in (forward, inverse, dft, idft))
    cosine, sine = jnp.asarray(cosine), jnp.asarray(sine)
    z, _, _ = position()

    def exchange(source, begin, count):
        size = (channels, HOP * count)
        out = {}
        for s in (*SHIFTS, 0):
            at = lax.rem(z + s, 4) * (SLICE * HOP) + begin * HOP
            part = lax.dynamic_slice(source, (0, at), size)
            out[s] = part if s == 0 else z_permute(part, s)
        return [out[s] for s in range(4)]

    halo = time_permute(record[:, :HOP], -1)
    raw = [exchange(record, 0, FR + 1)]
    own_mask = fan_mask.astype(BF).reshape(8, 256, 32).transpose(2, 0, 1)
    masks = [own_mask] + [z_permute(own_mask, s) for s in (1, 2, 3)]
    extended = jnp.concatenate([record, halo], axis=1)
    for i in range(1, CHUNKS):
        extended, _ = lax.optimization_barrier((extended, raw[-1]))
        raw.append(exchange(extended, FR * i + 1, FR))

    sums, carried = [], None
    for i in range(CHUNKS):
        spectra = stft(raw[i], None if i == 0 else raw[i - 1], forward)
        got = [spectra[0]] + [x_permute(spectra[j], *ROUTES[j]) for j in range(1, 8)]
        back = plane(got, masks, dft, idft, cosine, sine)
        got = [back[0]] + [x_permute(back[j], *ROUTES[j]) for j in range(1, 8)]
        last = i == CHUNKS - 1
        result = istft(got, inverse, carried, last)
        if not last:
            carried = result[4]
        sums.append([result[0]] + [z_permute(result[s], s) for s in (1, 2, 3)])

    ends = [a[:, HOP * FR :] for a in sums[-1]]
    edge = ends[3]
    for s in range(3):
        edge = jnp.where(lax.rem(z + 4 - s, 4) == 3, ends[s], edge)
    return join(sums, time_permute(edge, 1), span)


def solution(mesh):
    placed = (P("chan", "tm"), P("chan", None))
    return jax.shard_map(
        body, mesh=mesh, in_specs=placed, out_specs=P("chan", "tm"), check_vma=False
    )
```

```python
import functools

import jax
import jax.numpy as jnp
import numpy as np
from jax import lax
from jax.experimental import pallas as pl
from jax.experimental.pallas import tpu as pltpu
from jax.sharding import PartitionSpec as P


NCH = 8192
WIN = 512
HOP = 256
SLICE = 4
CHUNKS = (2, 2)
STARTS = tuple(sum(CHUNKS[:i]) for i in range(len(CHUNKS)))
BF = jnp.bfloat16
F32 = jnp.float32

ROUTES = [(0, 0), (2, 0), (2, 1), (1, 0), (1, 1), (3, 0), (3, 1), (0, 1)]
SHIFTS = (2, 1, 3)
HOLD = True


def make_tables():
    n = np.arange(WIN)
    w, zb, ri, b = np.meshgrid(np.arange(8), np.arange(4), np.arange(2), np.arange(8), indexing="ij")
    k = (64 * zb + 8 * w + b).reshape(8, 64, 1)
    imag = ri.reshape(8, 64, 1) == 1
    phase = ((k * n) % WIN) * (2.0 * np.pi / WIN)
    wave = np.where(imag, -np.sin(phase), np.cos(phase))
    taper = 0.5 - 0.5 * np.cos(n * (2.0 * np.pi / WIN))
    forward = wave * taper
    inverse = wave * np.where(k == 0, 1.0, 2.0) / (WIN * NCH)
    e = np.arange(256)
    turn = (np.outer(e, e) % 256) * (2.0 * np.pi / 256)
    dft = np.concatenate([np.cos(turn), -np.sin(turn)], axis=1)
    idft = np.concatenate([np.cos(turn), np.sin(turn)], axis=1)
    twist = np.outer(np.arange(32), e) * (2.0 * np.pi / NCH)
    return (
        forward.astype(jnp.bfloat16),
        inverse.reshape(512, WIN).astype(jnp.bfloat16),
        dft.astype(jnp.bfloat16),
        idft.astype(jnp.bfloat16),
        np.cos(twist).astype(np.float32),
        np.sin(twist).astype(np.float32),
    )


def position():
    d = lax.axis_index("chan")
    z = lax.div(d, 8)
    x = lax.rem(lax.div(d, 2), 4)
    k = lax.rem(d, 2)
    return z, x, k


def route_to(x, k, dx, dc):
    return 2 * lax.rem(x + dx, 4) + (k if dc == 0 else 1 - k)


def route_from(x, k, dx, dc):
    return 2 * lax.rem(x + 4 - dx, 4) + (k if dc == 0 else 1 - k)


def z_permute(value, shift):
    pairs = [(8 * z + w, 8 * ((z + shift) % 4) + w) for z in range(4) for w in range(8)]
    return lax.ppermute(value, "chan", pairs)


def x_permute(value, route):
    dx, dc = ROUTES[route]
    pairs = [
        (8 * z + 2 * x + k, 8 * z + 2 * ((x + dx) % 4) + (k ^ dc))
        for z in range(4)
        for x in range(4)
        for k in range(2)
    ]
    return lax.ppermute(value, "chan", pairs)


def end_permute(value, shift):
    peers = lax.axis_size("tm")
    pairs = [
        (32 * t + 8 * z + w, 32 * (t + (z == 3)) + 8 * ((z + shift) % 4) + w)
        for t in range(peers)
        for z in range(4)
        for w in range(8)
        if t + (z == 3) < peers
    ]
    return lax.ppermute(value, ("tm", "chan"), pairs)


def halo_permute(value):
    peers = lax.axis_size("tm")
    return lax.ppermute(value, "tm", [(i, i - 1) for i in range(1, peers)])


def cadd(a, b):
    return a[0] + b[0], a[1] + b[1]


def csub(a, b):
    return a[0] - b[0], a[1] - b[1]


def cturn(a, sign):
    return (-a[1], a[0]) if sign > 0 else (a[1], -a[0])


def cphase(a, num, den, sign):
    num = num % den
    if num == 0:
        return a
    if 4 * num == den:
        return cturn(a, sign)
    if 2 * num == den:
        return -a[0], -a[1]
    if 4 * num == 3 * den:
        return cturn(a, -sign)
    if 8 * num == den:
        h = np.float32(np.sqrt(0.5))
        t = cturn(a, sign)
        return (a[0] + t[0]) * h, (a[1] + t[1]) * h
    if 8 * num == 3 * den:
        h = np.float32(np.sqrt(0.5))
        t = cturn(a, sign)
        return (t[0] - a[0]) * h, (t[1] - a[1]) * h
    c = np.float32(np.cos(2 * np.pi * num / den))
    s = np.float32(sign * np.sin(2 * np.pi * num / den))
    return a[0] * c - a[1] * s, a[0] * s + a[1] * c


def dft4(v, sign):
    p, q = cadd(v[0], v[2]), csub(v[0], v[2])
    r, t = cadd(v[1], v[3]), cturn(csub(v[1], v[3]), sign)
    return [cadd(p, r), cadd(q, t), csub(p, r), csub(q, t)]


def dft8(v, sign):
    even = dft4(v[0::2], sign)
    odd = [cphase(a, i, 8, sign) for i, a in enumerate(dft4(v[1::2], sign))]
    return [cadd(a, b) for a, b in zip(even, odd)] + [csub(a, b) for a, b in zip(even, odd)]


def split_tile(tile):
    wide = tile.astype(F32)
    return wide[:8], wide[8:]


def join_tile(pair):
    return jnp.concatenate(pair, axis=0).astype(BF)


def stft_kernel(FR, first, *refs):
    pieces, refs = refs[:4], refs[4:]
    if not first:
        edges, refs = refs[:4], refs[4:]
    table, refs = refs[0], refs[1:]
    outs, ordered = refs[:8], refs[8]
    z, x, k = position()
    for i, (dx, dc) in enumerate(ROUTES):
        ordered[64 * i : 64 * (i + 1), :] = table[route_to(x, k, dx, dc)]
    nt = (((1,), (1,)), ((), ()))
    for s in range(4):
        place = pl.ds(pl.multiple_of(lax.rem(z + 4 - s, 4) * 256, 256), 256)
        for f in range(FR):
            if first:
                got = lax.dot_general(
                    ordered[...], pieces[s][:, HOP * f : HOP * f + WIN], nt, preferred_element_type=F32
                )
            elif f == 0:
                got = lax.dot_general(
                    ordered[:, :HOP], edges[s][...], nt, preferred_element_type=F32
                ) + lax.dot_general(
                    ordered[:, HOP:], pieces[s][:, :HOP], nt, preferred_element_type=F32
                )
            else:
                got = lax.dot_general(
                    ordered[...],
                    pieces[s][:, HOP * (f - 1) : HOP * (f + 1)],
                    nt,
                    preferred_element_type=F32,
                )
            got = got.astype(BF)
            for i in range(8):
                outs[i][f, :, place] = got[64 * i : 64 * (i + 1)]


def stft(FR, pieces, edges, table):
    first = edges is None
    whole = lambda a: pl.BlockSpec(a.shape, lambda i: (0,) * a.ndim)
    specs = [whole(a) for a in pieces]
    if not first:
        last = edges[0].shape[1] // HOP - 1
        specs += [pl.BlockSpec((256, HOP), lambda i: (0, last)) for _ in edges]
    specs.append(whole(table))
    shape = jax.ShapeDtypeStruct((FR, 64, 1024), BF)
    return pl.pallas_call(
        functools.partial(stft_kernel, FR, first),
        grid=(1,),
        out_shape=[shape] * 8,
        in_specs=specs,
        out_specs=[pl.BlockSpec(shape.shape, lambda i: (0, 0, 0))] * 8,
        scratch_shapes=[pltpu.VMEM((512, WIN), BF)],
        cost_estimate=pl.CostEstimate(
            flops=2 * 512 * 512 * 1024 * FR, bytes_accessed=8 << 20, transcendentals=0
        ),
        name="stft",
    )(*pieces, *([] if first else edges), table)


def plane_kernel(FR, *refs):
    pieces, masks, refs = refs[:8], refs[8:12], refs[12:]
    dft, idft, cosine, sine = refs[:4]
    outs, refs = refs[4:12], refs[12:]
    grid, mixed, gate, sems = refs
    rows = FR * 64
    BATCH = 8 // FR
    z, x, k = position()
    gates = [
        pltpu.make_async_copy(masks[s], gate.at[lax.rem(z + 4 - s, 4)], sems.at[8 * FR + s])
        for s in range(4)
    ]
    copies = [
        [
            pltpu.make_async_copy(
                pieces[i].at[f], grid.at[route_from(x, k, dx, dc), f], sems.at[8 * f + i]
            )
            for i, (dx, dc) in enumerate(ROUTES)
        ]
        for f in range(FR)
    ]
    for copy in sum(copies, []) + gates:
        copy.start()

    def forward(step, _):
        f = lax.div(step, 8)
        part = lax.rem(lax.div(step, 2), 4)
        lanes = pl.multiple_of(lax.rem(step, 2) * 128, 128)
        row = pl.ds(pl.multiple_of(part * 16, 16), 16)
        cut = pl.ds(pl.multiple_of(f * 64 + part * 16, 16), 16)

        def get(zz, w):
            return split_tile(grid[w, f, row, pl.ds(zz * 256 + lanes, 128)])

        for low in range(2):
            one, two = [], []
            for w in range(8):
                v = [get(zz, w) for zz in range(4)]
                if low == 0:
                    p, q = cadd(v[0], v[2]), cadd(v[1], v[3])
                else:
                    p, q = csub(v[0], v[2]), cturn(csub(v[1], v[3]), -1)
                one.append(cphase(cadd(p, q), w * low, 32, -1))
                two.append(cphase(csub(p, q), w * (low + 2), 32, -1))
            for j4, line in ((low, one), (low + 2, two)):
                for j8, (re, im) in enumerate(dft8(line, -1)):
                    m0 = j4 + 4 * j8
                    c = cosine[m0 : m0 + 1, pl.ds(lanes, 128)]
                    s = sine[m0 : m0 + 1, pl.ds(lanes, 128)]
                    mixed[m0, cut, pl.ds(lanes, 128)] = join_tile((re * c + im * s, im * c - re * s))
        return 0

    for f in range(FR):
        for copy in copies[f]:
            copy.wait()
        lax.fori_loop(8 * f, 8 * f + 8, forward, 0)
    for copy in gates:
        copy.wait()

    def filter_rows(step, _):
        at = pl.multiple_of(step * BATCH, BATCH)
        stack = mixed[pl.ds(at, BATCH)].reshape(BATCH * rows, 256)
        spread = jnp.dot(stack, dft[...], preferred_element_type=F32)
        spread = spread.reshape(BATCH, FR, 4, 2, 8, 512)
        re = spread[:, :, :, 0, :, :256] - spread[:, :, :, 1, :, 256:]
        im = spread[:, :, :, 0, :, 256:] + spread[:, :, :, 1, :, :256]
        keep = jnp.stack([gate[:, at + i].astype(F32) for i in range(BATCH)])[:, None]
        stack = jnp.stack([re * keep, im * keep], axis=3).reshape(BATCH * rows, 256).astype(BF)
        spread = jnp.dot(stack, idft[...], preferred_element_type=F32)
        spread = spread.reshape(BATCH, FR * 4, 2, 8, 512)
        for i in range(BATCH):
            re = spread[i, :, 0, :, :256] - spread[i, :, 1, :, 256:]
            im = spread[i, :, 0, :, 256:] + spread[i, :, 1, :, :256]
            c = cosine[pl.ds(at + i, 1), :]
            s = sine[pl.ds(at + i, 1), :]
            mixed[at + i] = (
                jnp.stack([re * c - im * s, re * s + im * c], axis=1).reshape(rows, 256).astype(BF)
            )
        return 0

    lax.fori_loop(0, 32 // BATCH, filter_rows, 0)

    def backward(step, _):
        f = lax.div(step, 8)
        part = lax.rem(lax.div(step, 2), 4)
        lanes = pl.multiple_of(lax.rem(step, 2) * 128, 128)
        row = pl.ds(pl.multiple_of(part * 16, 16), 16)
        cut = pl.ds(pl.multiple_of(f * 64 + part * 16, 16), 16)
        for odd in range(2):
            lines = []
            for j4 in range(4):
                v = [split_tile(mixed[j4 + 4 * j8, cut, pl.ds(lanes, 128)]) for j8 in range(8)]
                if odd == 0:
                    u = [cadd(v[i], v[i + 4]) for i in range(4)]
                else:
                    u = [cphase(csub(v[i], v[i + 4]), i, 8, 1) for i in range(4)]
                lines.append(
                    [cphase(a, (2 * i + odd) * j4, 32, 1) for i, a in enumerate(dft4(u, 1))]
                )
            for i in range(4):
                for zz, pair in enumerate(dft4([lines[j4][i] for j4 in range(4)], 1)):
                    grid[2 * i + odd, f, row, pl.ds(zz * 256 + lanes, 128)] = join_tile(pair)
        return 0

    copies = []
    for f in range(FR):
        lax.fori_loop(8 * f, 8 * f + 8, backward, 0)
        for i, (dx, dc) in enumerate(ROUTES):
            copies.append(
                pltpu.make_async_copy(
                    grid.at[route_to(x, k, dx, dc), f], outs[i].at[f], sems.at[8 * f + i]
                )
            )
            copies[-1].start()
    for copy in copies:
        copy.wait()


def plane(FR, pieces, masks, dft, idft, cosine, sine):
    whole = lambda a: pl.BlockSpec(a.shape, lambda: (0,) * a.ndim)
    anywhere = pl.BlockSpec(memory_space=pl.ANY)
    shape = jax.ShapeDtypeStruct((FR, 64, 1024), BF)
    return pl.pallas_call(
        functools.partial(plane_kernel, FR),
        out_shape=[shape] * 8,
        in_specs=[anywhere] * 12 + [whole(a) for a in (dft, idft, cosine, sine)],
        out_specs=[anywhere] * 8,
        scratch_shapes=[
            pltpu.VMEM((8, FR, 64, 1024), BF),
            pltpu.VMEM((32, FR * 64, 256), BF),
            pltpu.VMEM((4, 32, 8, 256), BF),
            pltpu.SemaphoreType.DMA((8 * FR + 4,)),
        ],
        cost_estimate=pl.CostEstimate(
            flops=4 * 32 * FR * 64 * 256 * 512 * 2, bytes_accessed=16 << 20, transcendentals=0
        ),
        name="plane",
    )(*pieces, *masks, dft, idft, cosine, sine)


def istft_kernel(FR, first, last, *refs):
    pieces, refs = refs[:8], refs[8:]
    table, refs = refs[0], refs[1:]
    if not first:
        carried, refs = refs[0], refs[1:]
    outs, refs = refs[:4], refs[4:]
    if last:
        ends, refs = refs[:4], refs[4:]
    else:
        carry, refs = refs[0], refs[1:]
    grid, sems = refs
    z, x, k = position()
    copies = [
        pltpu.make_async_copy(pieces[i], grid.at[:, route_from(x, k, dx, dc)], sems.at[i])
        for i, (dx, dc) in enumerate(ROUTES)
    ]
    for copy in copies:
        copy.start()
    for copy in copies:
        copy.wait()
    tn = (((0,), (0,)), ((), ()))
    for s in range(4):
        place = pl.ds(pl.multiple_of(lax.rem(z + s, 4) * 256, 256), 256)
        tail = None if first else carried[s]
        for f in range(FR):
            bins = grid[f, :, :, place].reshape(512, 256)
            signal = lax.dot_general(bins, table[...], tn, preferred_element_type=F32)
            head = signal[:, :HOP]
            if tail is not None:
                head = head + tail
            outs[s][:, HOP * f : HOP * (f + 1)] = head.astype(BF)
            tail = signal[:, HOP:]
        if last:
            ends[s][...] = tail.astype(BF)
        else:
            carry[s] = tail


def istft(FR, pieces, table, carried, last):
    first = carried is None
    whole = lambda a: pl.BlockSpec(a.shape, lambda: (0,) * len(a.shape))
    anywhere = pl.BlockSpec(memory_space=pl.ANY)
    operands = [*pieces, table] + ([] if first else [carried])
    shapes = [jax.ShapeDtypeStruct((256, HOP * FR), BF)] * 4
    if last:
        shapes += [jax.ShapeDtypeStruct((256, HOP), BF)] * 4
    else:
        shapes.append(jax.ShapeDtypeStruct((4, 256, HOP), F32))
    return pl.pallas_call(
        functools.partial(istft_kernel, FR, first, last),
        out_shape=shapes,
        in_specs=[anywhere] * 8 + [whole(a) for a in operands[8:]],
        out_specs=[whole(a) for a in shapes],
        scratch_shapes=[pltpu.VMEM((FR, 8, 64, 1024), BF), pltpu.SemaphoreType.DMA((8,))],
        cost_estimate=pl.CostEstimate(
            flops=2 * 512 * 512 * 1024 * FR, bytes_accessed=8 << 20, transcendentals=0
        ),
        name="istft",
    )(*operands)


def join_kernel(*refs):
    count = 4 * len(CHUNKS)
    pieces, ends, out = refs[:count], refs[count : count + 4], refs[-1]
    z, _, _ = position()
    for s in range(4):
        source = lax.rem(z + 4 - s, 4)
        start = pl.multiple_of(source * (SLICE * HOP), SLICE * HOP)
        ahead = ends[(s + 1) % 4][...].astype(F32)
        for i, (begin, FR) in enumerate(zip(STARTS, CHUNKS)):
            block = pieces[4 * i + s][...].astype(F32)
            if i == 0:
                out[:, pl.ds(start, HOP)] = block[:, :HOP] + ahead
                if FR > 1:
                    out[:, pl.ds(start + HOP, HOP * (FR - 1))] = block[:, HOP:]
            else:
                out[:, pl.ds(start + HOP * begin, HOP * FR)] = block


def join(chunks, ends, span):
    pieces = [a for chunk in chunks for a in chunk] + ends
    rows = 64
    return pl.pallas_call(
        join_kernel,
        grid=(256 // rows,),
        out_shape=jax.ShapeDtypeStruct((256, span), F32),
        in_specs=[pl.BlockSpec((rows, a.shape[1]), lambda i: (i, 0)) for a in pieces],
        out_specs=pl.BlockSpec((rows, span), lambda i: (i, 0)),
        cost_estimate=pl.CostEstimate(flops=1 << 20, bytes_accessed=8 << 20, transcendentals=0),
        name="join",
    )(*pieces)


def steps(record, fan_mask):
    channels, span = record.shape
    forward, inverse, dft, idft, cosine, sine = (jnp.asarray(a) for a in make_tables())
    z, _, _ = position()

    def exchange(source, begin, count):
        size = (channels, HOP * count)
        out = {}
        for s in (*SHIFTS, 0):
            at = lax.rem(z + s, 4) * (SLICE * HOP) + begin * HOP
            part = lax.dynamic_slice(source, (0, at), size)
            out[s] = part if s == 0 else z_permute(part, s)
        return [out[s] for s in range(4)]

    raw = [exchange(record, 0, CHUNKS[0] + 1)]
    halo = halo_permute(record[:, :HOP])
    own_mask = fan_mask.astype(BF).reshape(8, 256, 32).transpose(2, 0, 1)
    masks = [own_mask] + [z_permute(own_mask, s) for s in (1, 2, 3)]
    extended = jnp.concatenate([record, halo], axis=1)
    for i in range(1, len(CHUNKS)):
        source = extended if i == len(CHUNKS) - 1 else record
        if HOLD:
            source, _ = lax.optimization_barrier((source, raw[-1]))
        raw.append(exchange(source, STARTS[i] + 1, CHUNKS[i]))

    sums, carried = [], None
    for i, frames in enumerate(CHUNKS):
        spectra = stft(frames, raw[i], None if i == 0 else raw[i - 1], forward)
        got = [spectra[0]] + [x_permute(spectra[j], j) for j in range(1, 8)]
        back = plane(frames, got, masks, dft, idft, cosine, sine)
        got = [back[0]] + [x_permute(back[j], j) for j in range(1, 8)]
        last = i == len(CHUNKS) - 1
        result = istft(frames, got, inverse, carried, last)
        sums.append([result[0]] + [z_permute(result[s], s) for s in (1, 2, 3)])
        carried = result[4]
    ends = [end_permute(result[4 + s], s) for s in range(4)]
    return join(sums, ends, span)


def solution(mesh):
    placed = (P("chan", "tm"), P("chan", None))
    return jax.shard_map(
        steps, mesh=mesh, in_specs=placed, out_specs=P("chan", "tm"), check_vma=False
    )
```

```python
import functools

import jax
import jax.numpy as jnp
import numpy as np
from jax import lax
from jax.experimental import pallas as pl
from jax.experimental.pallas import tpu as pltpu
from jax.sharding import PartitionSpec as P


NCH = 8192
WIN = 512
HOP = 256
SLICE = 4
CHUNKS = (2, 2)
STARTS = tuple(sum(CHUNKS[:i]) for i in range(len(CHUNKS)))
BF = jnp.bfloat16
F32 = jnp.float32

ROUTES = [(0, 0), (2, 0), (2, 1), (1, 0), (1, 1), (3, 0), (3, 1), (0, 1)]
SHIFTS = (2, 1, 3)
HOLD = (1, 3)


def make_tables():
    n = np.arange(WIN)
    w, zb, ri, b = np.meshgrid(np.arange(8), np.arange(4), np.arange(2), np.arange(8), indexing="ij")
    k = (64 * zb + 8 * w + b).reshape(8, 64, 1)
    imag = ri.reshape(8, 64, 1) == 1
    phase = ((k * n) % WIN) * (2.0 * np.pi / WIN)
    wave = np.where(imag, -np.sin(phase), np.cos(phase))
    taper = 0.5 - 0.5 * np.cos(n * (2.0 * np.pi / WIN))
    forward = wave * taper
    inverse = wave * np.where(k == 0, 1.0, 2.0) / (WIN * NCH)
    e = np.arange(256)
    turn = (np.outer(e, e) % 256) * (2.0 * np.pi / 256)
    dft = np.concatenate([np.cos(turn), -np.sin(turn)], axis=1)
    idft = np.concatenate([np.cos(turn), np.sin(turn)], axis=1)
    twist = np.outer(np.arange(32), e) * (2.0 * np.pi / NCH)
    return (
        forward.astype(jnp.bfloat16),
        inverse.reshape(512, WIN).astype(jnp.bfloat16),
        dft.astype(jnp.bfloat16),
        idft.astype(jnp.bfloat16),
        np.cos(twist).astype(np.float32),
        np.sin(twist).astype(np.float32),
    )


def position():
    d = lax.axis_index("chan")
    z = lax.div(d, 8)
    x = lax.rem(lax.div(d, 2), 4)
    k = lax.rem(d, 2)
    return z, x, k


def route_to(x, k, dx, dc):
    return 2 * lax.rem(x + dx, 4) + (k if dc == 0 else 1 - k)


def route_from(x, k, dx, dc):
    return 2 * lax.rem(x + 4 - dx, 4) + (k if dc == 0 else 1 - k)


def z_permute(value, shift):
    pairs = [(8 * z + w, 8 * ((z + shift) % 4) + w) for z in range(4) for w in range(8)]
    return lax.ppermute(value, "chan", pairs)


def x_permute(value, route):
    dx, dc = ROUTES[route]
    pairs = [
        (8 * z + 2 * x + k, 8 * z + 2 * ((x + dx) % 4) + (k ^ dc))
        for z in range(4)
        for x in range(4)
        for k in range(2)
    ]
    return lax.ppermute(value, "chan", pairs)


def end_permute(value, shift):
    peers = lax.axis_size("tm")
    pairs = [
        (32 * t + 8 * z + w, 32 * (t + (z == 3)) + 8 * ((z + shift) % 4) + w)
        for t in range(peers)
        for z in range(4)
        for w in range(8)
        if t + (z == 3) < peers
    ]
    return lax.ppermute(value, ("tm", "chan"), pairs)


def y_permute(value, shift):
    peers = lax.axis_size("tm")
    pairs = [(t, (t + 2 * shift) % peers) for t in range(peers)]
    return lax.ppermute(value, "tm", pairs)


def gather_masks(own):
    y = lax.div(lax.axis_index("tm"), 2)
    quarter = lax.dynamic_slice(own, (8 * y, 0, 0), (8, 8, 256))
    part = jnp.stack([z_permute(quarter, s) for s in (1, 2, 3)])
    return [own, part] + [y_permute(part, j) for j in (1, 2, 3)]


def halo_permute(value):
    peers = lax.axis_size("tm")
    return lax.ppermute(value, "tm", [(i, i - 1) for i in range(1, peers)])


def cadd(a, b):
    return a[0] + b[0], a[1] + b[1]


def csub(a, b):
    return a[0] - b[0], a[1] - b[1]


def cturn(a, sign):
    return (-a[1], a[0]) if sign > 0 else (a[1], -a[0])


def cphase(a, num, den, sign):
    num = num % den
    if num == 0:
        return a
    if 4 * num == den:
        return cturn(a, sign)
    if 2 * num == den:
        return -a[0], -a[1]
    if 4 * num == 3 * den:
        return cturn(a, -sign)
    if 8 * num == den:
        h = np.float32(np.sqrt(0.5))
        t = cturn(a, sign)
        return (a[0] + t[0]) * h, (a[1] + t[1]) * h
    if 8 * num == 3 * den:
        h = np.float32(np.sqrt(0.5))
        t = cturn(a, sign)
        return (t[0] - a[0]) * h, (t[1] - a[1]) * h
    c = np.float32(np.cos(2 * np.pi * num / den))
    s = np.float32(sign * np.sin(2 * np.pi * num / den))
    return a[0] * c - a[1] * s, a[0] * s + a[1] * c


def dft4(v, sign):
    p, q = cadd(v[0], v[2]), csub(v[0], v[2])
    r, t = cadd(v[1], v[3]), cturn(csub(v[1], v[3]), sign)
    return [cadd(p, r), cadd(q, t), csub(p, r), csub(q, t)]


def dft8(v, sign):
    even = dft4(v[0::2], sign)
    odd = [cphase(a, i, 8, sign) for i, a in enumerate(dft4(v[1::2], sign))]
    return [cadd(a, b) for a, b in zip(even, odd)] + [csub(a, b) for a, b in zip(even, odd)]


def split_tile(tile):
    wide = tile.astype(F32)
    return wide[:8], wide[8:]


def join_tile(pair):
    return jnp.concatenate(pair, axis=0).astype(BF)


def stft_kernel(FR, first, *refs):
    pieces, refs = refs[:4], refs[4:]
    if not first:
        edges, refs = refs[:4], refs[4:]
    table, refs = refs[0], refs[1:]
    outs, ordered = refs[:8], refs[8]
    z, x, k = position()
    for i, (dx, dc) in enumerate(ROUTES):
        ordered[64 * i : 64 * (i + 1), :] = table[route_to(x, k, dx, dc)]
    nt = (((1,), (1,)), ((), ()))
    for s in range(4):
        place = pl.ds(pl.multiple_of(lax.rem(z + 4 - s, 4) * 256, 256), 256)
        for f in range(FR):
            if first:
                got = lax.dot_general(
                    ordered[...], pieces[s][:, HOP * f : HOP * f + WIN], nt, preferred_element_type=F32
                )
            elif f == 0:
                got = lax.dot_general(
                    ordered[:, :HOP], edges[s][...], nt, preferred_element_type=F32
                ) + lax.dot_general(
                    ordered[:, HOP:], pieces[s][:, :HOP], nt, preferred_element_type=F32
                )
            else:
                got = lax.dot_general(
                    ordered[...],
                    pieces[s][:, HOP * (f - 1) : HOP * (f + 1)],
                    nt,
                    preferred_element_type=F32,
                )
            got = got.astype(BF)
            for i in range(8):
                outs[i][f, :, place] = got[64 * i : 64 * (i + 1)]


def stft(FR, pieces, edges, table):
    first = edges is None
    whole = lambda a: pl.BlockSpec(a.shape, lambda i: (0,) * a.ndim)
    specs = [whole(a) for a in pieces]
    if not first:
        last = edges[0].shape[1] // HOP - 1
        specs += [pl.BlockSpec((256, HOP), lambda i: (0, last)) for _ in edges]
    specs.append(whole(table))
    shape = jax.ShapeDtypeStruct((FR, 64, 1024), BF)
    return pl.pallas_call(
        functools.partial(stft_kernel, FR, first),
        grid=(1,),
        out_shape=[shape] * 8,
        in_specs=specs,
        out_specs=[pl.BlockSpec(shape.shape, lambda i: (0, 0, 0))] * 8,
        scratch_shapes=[pltpu.VMEM((512, WIN), BF)],
        cost_estimate=pl.CostEstimate(
            flops=2 * 512 * 512 * 1024 * FR, bytes_accessed=8 << 20, transcendentals=0
        ),
        name="stft",
    )(*pieces, *([] if first else edges), table)


def local_stft_kernel(FR, begin, record, halo, table, *refs):
    outs, ordered = refs[:8], refs[8]
    _, x, k = position()
    for i, (dx, dc) in enumerate(ROUTES):
        ordered[64 * i : 64 * (i + 1), :] = table[route_to(x, k, dx, dc)]
    nt = (((1,), (1,)), ((), ()))
    hops = record.shape[1] // HOP
    for part in range(4):
        for f in range(FR):
            hop = SLICE * part + begin + f
            if hop + 1 < hops:
                got = lax.dot_general(
                    ordered[...],
                    record[:, HOP * hop : HOP * hop + WIN],
                    nt,
                    preferred_element_type=F32,
                )
            else:
                got = lax.dot_general(
                    ordered[:, :HOP], record[:, HOP * hop :], nt, preferred_element_type=F32
                ) + lax.dot_general(
                    ordered[:, HOP:], halo[...], nt, preferred_element_type=F32
                )
            got = got.astype(BF)
            for i in range(8):
                outs[i][part, f] = got[64 * i : 64 * (i + 1)]


def local_stft(FR, begin, record, halo, table):
    whole = lambda a: pl.BlockSpec(a.shape, lambda i: (0,) * len(a.shape))
    shape = jax.ShapeDtypeStruct((4, FR, 64, 256), BF)
    return pl.pallas_call(
        functools.partial(local_stft_kernel, FR, begin),
        grid=(1,),
        out_shape=[shape] * 8,
        in_specs=[whole(a) for a in (record, halo, table)],
        out_specs=[whole(shape)] * 8,
        scratch_shapes=[pltpu.VMEM((512, WIN), BF)],
        cost_estimate=pl.CostEstimate(
            flops=2 * 512 * 512 * 1024 * FR, bytes_accessed=8 << 20, transcendentals=0
        ),
        name="local_stft",
    )(record, halo, table)


def repack_kernel(*refs):
    pieces, outs, (grid, sems) = refs[:8], refs[8:12], refs[12:]
    z, x, k = position()
    copies = [
        pltpu.make_async_copy(pieces[i], grid.at[route_from(x, k, dx, dc)], sems.at[i])
        for i, (dx, dc) in enumerate(ROUTES)
    ]
    for copy in copies:
        copy.start()
    for copy in copies:
        copy.wait()
    copies = [
        pltpu.make_async_copy(grid.at[:, lax.rem(z + s, 4)], outs[s], sems.at[s])
        for s in range(4)
    ]
    for copy in copies:
        copy.start()
    for copy in copies:
        copy.wait()


def repack(pieces):
    _, frames, rows, lanes = pieces[0].shape
    anywhere = pl.BlockSpec(memory_space=pl.ANY)
    return pl.pallas_call(
        repack_kernel,
        out_shape=[jax.ShapeDtypeStruct((8, frames, rows, lanes), BF)] * 4,
        in_specs=[anywhere] * 8,
        out_specs=[anywhere] * 4,
        scratch_shapes=[
            pltpu.VMEM((8, 4, frames, rows, lanes), BF),
            pltpu.SemaphoreType.DMA((8,)),
        ],
        cost_estimate=pl.CostEstimate(flops=1 << 20, bytes_accessed=4 << 20, transcendentals=0),
        name="repack",
    )(*pieces)


def plane_kernel(FR, x_first, *refs):
    count = 4 if x_first else 8
    pieces, masks, refs = refs[:count], refs[count : count + 5], refs[count + 5 :]
    dft, idft, cosine, sine = refs[:4]
    outs, refs = refs[4:12], refs[12:]
    if x_first:
        grid, mixed, gate, sems, source = refs
    else:
        grid, mixed, gate, sems = refs
    rows = FR * 64
    BATCH = 16 // FR
    z, x, k = position()
    y = lax.div(lax.axis_index("tm"), 2)
    gates = [pltpu.make_async_copy(masks[0], gate.at[z], sems.at[8 * FR])]
    for j in range(4):
        low = pl.ds(pl.multiple_of(lax.rem(y + 4 - j, 4) * 8, 8), 8)
        for s in (1, 2, 3):
            gates.append(
                pltpu.make_async_copy(
                    masks[1 + j].at[s - 1],
                    gate.at[lax.rem(z + 4 - s, 4), low],
                    sems.at[8 * FR + 3 * j + s],
                )
            )
    if x_first:
        copies = [
            [
                pltpu.make_async_copy(
                    pieces[i].at[:, f], source.at[lax.rem(z + 4 - i, 4), :, f], sems.at[8 * f + i]
                )
                for i in range(4)
            ]
            for f in range(FR)
        ]
    else:
        copies = [
            [
                pltpu.make_async_copy(
                    pieces[i].at[f], grid.at[route_from(x, k, dx, dc), f], sems.at[8 * f + i]
                )
                for i, (dx, dc) in enumerate(ROUTES)
            ]
            for f in range(FR)
        ]
    for copy in sum(copies, []) + gates:
        copy.start()

    def forward(step, _):
        f = lax.div(step, 8)
        part = lax.rem(lax.div(step, 2), 4)
        lanes = pl.multiple_of(lax.rem(step, 2) * 128, 128)
        row = pl.ds(pl.multiple_of(part * 16, 16), 16)
        cut = pl.ds(pl.multiple_of(f * 64 + part * 16, 16), 16)

        def get(zz, w):
            if x_first:
                return split_tile(source[zz, w, f, row, pl.ds(lanes, 128)])
            return split_tile(grid[w, f, row, pl.ds(zz * 256 + lanes, 128)])

        for low in range(2):
            one, two = [], []
            for w in range(8):
                v = [get(zz, w) for zz in range(4)]
                if low == 0:
                    p, q = cadd(v[0], v[2]), cadd(v[1], v[3])
                else:
                    p, q = csub(v[0], v[2]), cturn(csub(v[1], v[3]), -1)
                one.append(cphase(cadd(p, q), w * low, 32, -1))
                two.append(cphase(csub(p, q), w * (low + 2), 32, -1))
            for j4, line in ((low, one), (low + 2, two)):
                for j8, (re, im) in enumerate(dft8(line, -1)):
                    m0 = j4 + 4 * j8
                    c = cosine[m0 : m0 + 1, pl.ds(lanes, 128)]
                    s = sine[m0 : m0 + 1, pl.ds(lanes, 128)]
                    mixed[m0, cut, pl.ds(lanes, 128)] = join_tile((re * c + im * s, im * c - re * s))
        return 0

    for f in range(FR):
        for copy in copies[f]:
            copy.wait()
        lax.fori_loop(8 * f, 8 * f + 8, forward, 0)
    for copy in gates:
        copy.wait()

    def filter_rows(step, _):
        at = pl.multiple_of(step * BATCH, BATCH)
        stack = mixed[pl.ds(at, BATCH)].reshape(BATCH * rows, 256)
        spread = jnp.dot(stack, dft[...], preferred_element_type=F32)
        spread = spread.reshape(BATCH, FR, 4, 2, 8, 512)
        re = spread[:, :, :, 0, :, :256] - spread[:, :, :, 1, :, 256:]
        im = spread[:, :, :, 0, :, 256:] + spread[:, :, :, 1, :, :256]
        keep = jnp.stack([gate[:, at + i].astype(F32) for i in range(BATCH)])[:, None]
        stack = jnp.stack([re * keep, im * keep], axis=3).reshape(BATCH * rows, 256).astype(BF)
        spread = jnp.dot(stack, idft[...], preferred_element_type=F32)
        spread = spread.reshape(BATCH, FR * 4, 2, 8, 512)
        for i in range(BATCH):
            re = spread[i, :, 0, :, :256] - spread[i, :, 1, :, 256:]
            im = spread[i, :, 0, :, 256:] + spread[i, :, 1, :, :256]
            c = cosine[pl.ds(at + i, 1), :]
            s = sine[pl.ds(at + i, 1), :]
            mixed[at + i] = (
                jnp.stack([re * c - im * s, re * s + im * c], axis=1).reshape(rows, 256).astype(BF)
            )
        return 0

    lax.fori_loop(0, 32 // BATCH, filter_rows, 0)

    def backward(step, _):
        f = lax.div(step, 8)
        part = lax.rem(lax.div(step, 2), 4)
        lanes = pl.multiple_of(lax.rem(step, 2) * 128, 128)
        row = pl.ds(pl.multiple_of(part * 16, 16), 16)
        cut = pl.ds(pl.multiple_of(f * 64 + part * 16, 16), 16)
        for odd in range(2):
            lines = []
            for j4 in range(4):
                v = [split_tile(mixed[j4 + 4 * j8, cut, pl.ds(lanes, 128)]) for j8 in range(8)]
                if odd == 0:
                    u = [cadd(v[i], v[i + 4]) for i in range(4)]
                else:
                    u = [cphase(csub(v[i], v[i + 4]), i, 8, 1) for i in range(4)]
                lines.append(
                    [cphase(a, (2 * i + odd) * j4, 32, 1) for i, a in enumerate(dft4(u, 1))]
                )
            for i in range(4):
                for zz, pair in enumerate(dft4([lines[j4][i] for j4 in range(4)], 1)):
                    grid[2 * i + odd, f, row, pl.ds(zz * 256 + lanes, 128)] = join_tile(pair)
        return 0

    copies = []
    for f in range(FR):
        lax.fori_loop(8 * f, 8 * f + 8, backward, 0)
        for i, (dx, dc) in enumerate(ROUTES):
            copies.append(
                pltpu.make_async_copy(
                    grid.at[route_to(x, k, dx, dc), f], outs[i].at[f], sems.at[8 * f + i]
                )
            )
            copies[-1].start()
    for copy in copies:
        copy.wait()


def plane(FR, x_first, pieces, masks, dft, idft, cosine, sine):
    whole = lambda a: pl.BlockSpec(a.shape, lambda: (0,) * a.ndim)
    anywhere = pl.BlockSpec(memory_space=pl.ANY)
    shape = jax.ShapeDtypeStruct((FR, 64, 1024), BF)
    return pl.pallas_call(
        functools.partial(plane_kernel, FR, x_first),
        out_shape=[shape] * 8,
        in_specs=[anywhere] * (len(pieces) + 5) + [whole(a) for a in (dft, idft, cosine, sine)],
        out_specs=[anywhere] * 8,
        scratch_shapes=[
            pltpu.VMEM((8, FR, 64, 1024), BF),
            pltpu.VMEM((32, FR * 64, 256), BF),
            pltpu.VMEM((4, 32, 8, 256), BF),
            pltpu.SemaphoreType.DMA((8 * FR + 13,)),
        ]
        + ([pltpu.VMEM((4, 8, FR, 64, 256), BF)] if x_first else []),
        cost_estimate=pl.CostEstimate(
            flops=4 * 32 * FR * 64 * 256 * 512 * 2, bytes_accessed=16 << 20, transcendentals=0
        ),
        name="plane",
    )(*pieces, *masks, dft, idft, cosine, sine)


def istft_kernel(FR, first, last, *refs):
    pieces, refs = refs[:8], refs[8:]
    table, refs = refs[0], refs[1:]
    if not first:
        carried, refs = refs[0], refs[1:]
    outs, refs = refs[:4], refs[4:]
    if last:
        ends, refs = refs[:4], refs[4:]
    else:
        carry, refs = refs[0], refs[1:]
    grid, sems = refs
    z, x, k = position()
    copies = [
        pltpu.make_async_copy(pieces[i], grid.at[:, route_from(x, k, dx, dc)], sems.at[i])
        for i, (dx, dc) in enumerate(ROUTES)
    ]
    for copy in copies:
        copy.start()
    for copy in copies:
        copy.wait()
    tn = (((0,), (0,)), ((), ()))
    for s in range(4):
        place = pl.ds(pl.multiple_of(lax.rem(z + s, 4) * 256, 256), 256)
        tail = None if first else carried[s]
        for f in range(FR):
            bins = grid[f, :, :, place].reshape(512, 256)
            signal = lax.dot_general(bins, table[...], tn, preferred_element_type=F32)
            head = signal[:, :HOP]
            if tail is not None:
                head = head + tail
            outs[s][:, HOP * f : HOP * (f + 1)] = head.astype(BF)
            tail = signal[:, HOP:]
        if last:
            ends[s][...] = tail.astype(BF)
        else:
            carry[s] = tail


def istft(FR, pieces, table, carried, last):
    first = carried is None
    whole = lambda a: pl.BlockSpec(a.shape, lambda: (0,) * len(a.shape))
    anywhere = pl.BlockSpec(memory_space=pl.ANY)
    operands = [*pieces, table] + ([] if first else [carried])
    shapes = [jax.ShapeDtypeStruct((256, HOP * FR), BF)] * 4
    if last:
        shapes += [jax.ShapeDtypeStruct((256, HOP), BF)] * 4
    else:
        shapes.append(jax.ShapeDtypeStruct((4, 256, HOP), F32))
    return pl.pallas_call(
        functools.partial(istft_kernel, FR, first, last),
        out_shape=shapes,
        in_specs=[anywhere] * 8 + [whole(a) for a in operands[8:]],
        out_specs=[whole(a) for a in shapes],
        scratch_shapes=[pltpu.VMEM((FR, 8, 64, 1024), BF), pltpu.SemaphoreType.DMA((8,))],
        cost_estimate=pl.CostEstimate(
            flops=2 * 512 * 512 * 1024 * FR, bytes_accessed=8 << 20, transcendentals=0
        ),
        name="istft",
    )(*operands)


def join_kernel(*refs):
    count = 4 * len(CHUNKS)
    pieces, ends, out = refs[:count], refs[count : count + 4], refs[-1]
    z, _, _ = position()
    for s in range(4):
        source = lax.rem(z + 4 - s, 4)
        start = pl.multiple_of(source * (SLICE * HOP), SLICE * HOP)
        ahead = ends[(s + 1) % 4][...].astype(F32)
        for i, (begin, FR) in enumerate(zip(STARTS, CHUNKS)):
            block = pieces[4 * i + s][...].astype(F32)
            if i == 0:
                out[:, pl.ds(start, HOP)] = block[:, :HOP] + ahead
                if FR > 1:
                    out[:, pl.ds(start + HOP, HOP * (FR - 1))] = block[:, HOP:]
            else:
                out[:, pl.ds(start + HOP * begin, HOP * FR)] = block


def join(chunks, ends, span):
    pieces = [a for chunk in chunks for a in chunk] + ends
    rows = 64
    return pl.pallas_call(
        join_kernel,
        grid=(256 // rows,),
        out_shape=jax.ShapeDtypeStruct((256, span), F32),
        in_specs=[pl.BlockSpec((rows, a.shape[1]), lambda i: (i, 0)) for a in pieces],
        out_specs=pl.BlockSpec((rows, span), lambda i: (i, 0)),
        cost_estimate=pl.CostEstimate(flops=1 << 20, bytes_accessed=8 << 20, transcendentals=0),
        name="join",
    )(*pieces)


def steps(record, fan_mask):
    channels, span = record.shape
    forward, inverse, dft, idft, cosine, sine = (jnp.asarray(a) for a in make_tables())
    z, _, _ = position()

    def exchange(source, begin, count):
        size = (channels, HOP * count)
        out = {}
        for s in (*SHIFTS, 0):
            at = lax.rem(z + s, 4) * (SLICE * HOP) + begin * HOP
            part = lax.dynamic_slice(source, (0, at), size)
            out[s] = part if s == 0 else z_permute(part, s)
        return [out[s] for s in range(4)]

    halo = halo_permute(record[:, :HOP])
    raw = exchange(record, 0, CHUNKS[0] + 1)
    spectra = local_stft(CHUNKS[1], STARTS[1], record, halo, forward)
    got = [spectra[0]] + [x_permute(spectra[j], j) for j in range(1, 8)]
    own_mask = fan_mask.astype(BF).reshape(8, 256, 32).transpose(2, 0, 1)
    packed = repack(got)
    packed, _ = lax.optimization_barrier((packed, [raw[j] for j in HOLD]))
    second = [packed[0]] + [z_permute(packed[s], s) for s in (1, 2, 3)]
    masks = gather_masks(own_mask)

    spectra = stft(CHUNKS[0], raw, None, forward)
    first = [spectra[0]] + [x_permute(spectra[j], j) for j in range(1, 8)]

    sums, carried = [], None
    for i, frames in enumerate(CHUNKS):
        back = plane(frames, i == 1, (first, second)[i], masks, dft, idft, cosine, sine)
        got = [back[0]] + [x_permute(back[j], j) for j in range(1, 8)]
        last = i == len(CHUNKS) - 1
        result = istft(frames, got, inverse, carried, last)
        sums.append([result[0]] + [z_permute(result[s], s) for s in (1, 2, 3)])
        carried = result[4]
    ends = [end_permute(result[4 + s], s) for s in range(4)]
    return join(sums, ends, span)


def solution(mesh):
    placed = (P("chan", "tm"), P("chan", None))
    return jax.shard_map(
        steps, mesh=mesh, in_specs=placed, out_specs=P("chan", "tm"), check_vma=False
    )
```

```python
import functools

import jax
import jax.numpy as jnp
import numpy as np
from jax import lax
from jax.experimental import pallas as pl
from jax.experimental.pallas import tpu as pltpu
from jax.sharding import PartitionSpec as P


NCH = 8192
WIN = 512
HOP = 256
SLICE = 4
CHUNKS = (2, 2)
STARTS = tuple(sum(CHUNKS[:i]) for i in range(len(CHUNKS)))
BF = jnp.bfloat16
F32 = jnp.float32

ROUTES = [(0, 0), (2, 0), (2, 1), (1, 0), (1, 1), (3, 0), (3, 1), (0, 1)]
SHIFTS = (2, 1, 3)
HOLD = (1, 3)


def make_tables():
    n = np.arange(WIN)
    w, zb, ri, b = np.meshgrid(np.arange(8), np.arange(4), np.arange(2), np.arange(8), indexing="ij")
    k = (64 * zb + 8 * w + b).reshape(8, 64, 1)
    imag = ri.reshape(8, 64, 1) == 1
    phase = ((k * n) % WIN) * (2.0 * np.pi / WIN)
    wave = np.where(imag, -np.sin(phase), np.cos(phase))
    taper = 0.5 - 0.5 * np.cos(n * (2.0 * np.pi / WIN))
    e = np.arange(256)
    turn = (np.outer(e, e) % 256) * (2.0 * np.pi / 256)
    dft = np.concatenate([np.cos(turn), -np.sin(turn)], axis=1)
    twist = np.outer(np.arange(32), e) * (2.0 * np.pi / NCH)
    return (
        wave.astype(jnp.bfloat16),
        taper.reshape(1, WIN).astype(np.float32),
        dft.astype(jnp.bfloat16),
        np.cos(twist).astype(np.float32),
        np.sin(twist).astype(np.float32),
    )


def position():
    d = lax.axis_index("chan")
    z = lax.div(d, 8)
    x = lax.rem(lax.div(d, 2), 4)
    k = lax.rem(d, 2)
    return z, x, k


def route_to(x, k, dx, dc):
    return 2 * lax.rem(x + dx, 4) + (k if dc == 0 else 1 - k)


def route_from(x, k, dx, dc):
    return 2 * lax.rem(x + 4 - dx, 4) + (k if dc == 0 else 1 - k)


def z_permute(value, shift):
    pairs = [(8 * z + w, 8 * ((z + shift) % 4) + w) for z in range(4) for w in range(8)]
    return lax.ppermute(value, "chan", pairs)


def x_permute(value, route):
    dx, dc = ROUTES[route]
    pairs = [
        (8 * z + 2 * x + k, 8 * z + 2 * ((x + dx) % 4) + (k ^ dc))
        for z in range(4)
        for x in range(4)
        for k in range(2)
    ]
    return lax.ppermute(value, "chan", pairs)


def end_permute(value, shift):
    peers = lax.axis_size("tm")
    pairs = [
        (32 * t + 8 * z + w, 32 * (t + (z == 3)) + 8 * ((z + shift) % 4) + w)
        for t in range(peers)
        for z in range(4)
        for w in range(8)
        if t + (z == 3) < peers
    ]
    return lax.ppermute(value, ("tm", "chan"), pairs)


def y_permute(value, shift):
    peers = lax.axis_size("tm")
    pairs = [(t, (t + 2 * shift) % peers) for t in range(peers)]
    return lax.ppermute(value, "tm", pairs)


def gather_masks(own):
    y = lax.div(lax.axis_index("tm"), 2)
    quarter = lax.dynamic_slice(own, (8 * y, 0, 0), (8, 8, 256))
    part = jnp.stack([z_permute(quarter, s) for s in (1, 2, 3)])
    return [own, part] + [y_permute(part, j) for j in (1, 2, 3)]


def halo_permute(value):
    peers = lax.axis_size("tm")
    return lax.ppermute(value, "tm", [(i, i - 1) for i in range(1, peers)])


def cadd(a, b):
    return a[0] + b[0], a[1] + b[1]


def csub(a, b):
    return a[0] - b[0], a[1] - b[1]


def cturn(a, sign):
    return (-a[1], a[0]) if sign > 0 else (a[1], -a[0])


def cphase(a, num, den, sign):
    num = num % den
    if num == 0:
        return a
    if 4 * num == den:
        return cturn(a, sign)
    if 2 * num == den:
        return -a[0], -a[1]
    if 4 * num == 3 * den:
        return cturn(a, -sign)
    if 8 * num == den:
        h = np.float32(np.sqrt(0.5))
        t = cturn(a, sign)
        return (a[0] + t[0]) * h, (a[1] + t[1]) * h
    if 8 * num == 3 * den:
        h = np.float32(np.sqrt(0.5))
        t = cturn(a, sign)
        return (t[0] - a[0]) * h, (t[1] - a[1]) * h
    c = np.float32(np.cos(2 * np.pi * num / den))
    s = np.float32(sign * np.sin(2 * np.pi * num / den))
    return a[0] * c - a[1] * s, a[0] * s + a[1] * c


def dft4(v, sign):
    p, q = cadd(v[0], v[2]), csub(v[0], v[2])
    r, t = cadd(v[1], v[3]), cturn(csub(v[1], v[3]), sign)
    return [cadd(p, r), cadd(q, t), csub(p, r), csub(q, t)]


def dft8(v, sign):
    even = dft4(v[0::2], sign)
    odd = [cphase(a, i, 8, sign) for i, a in enumerate(dft4(v[1::2], sign))]
    return [cadd(a, b) for a, b in zip(even, odd)] + [csub(a, b) for a, b in zip(even, odd)]


def split_tile(tile):
    wide = tile.astype(F32)
    return wide[:8], wide[8:]


def join_tile(pair):
    return jnp.concatenate(pair, axis=0).astype(BF)


def stft_kernel(FR, first, *refs):
    pieces, refs = refs[:4], refs[4:]
    if not first:
        edges, refs = refs[:4], refs[4:]
    table, taper, refs = refs[0], refs[1], refs[2:]
    outs, ordered = refs[:8], refs[8]
    z, x, k = position()
    for i, (dx, dc) in enumerate(ROUTES):
        rows = table[route_to(x, k, dx, dc)].astype(F32)
        ordered[64 * i : 64 * (i + 1), :] = (rows * taper[...]).astype(BF)
    nt = (((1,), (1,)), ((), ()))
    for s in range(4):
        place = pl.ds(pl.multiple_of(lax.rem(z + 4 - s, 4) * 256, 256), 256)
        for f in range(FR):
            if first:
                got = lax.dot_general(
                    ordered[...], pieces[s][:, HOP * f : HOP * f + WIN], nt, preferred_element_type=F32
                )
            elif f == 0:
                got = lax.dot_general(
                    ordered[:, :HOP], edges[s][...], nt, preferred_element_type=F32
                ) + lax.dot_general(
                    ordered[:, HOP:], pieces[s][:, :HOP], nt, preferred_element_type=F32
                )
            else:
                got = lax.dot_general(
                    ordered[...],
                    pieces[s][:, HOP * (f - 1) : HOP * (f + 1)],
                    nt,
                    preferred_element_type=F32,
                )
            got = got.astype(BF)
            for i in range(8):
                outs[i][f, :, place] = got[64 * i : 64 * (i + 1)]


def stft(FR, pieces, edges, table, taper):
    first = edges is None
    whole = lambda a: pl.BlockSpec(a.shape, lambda i: (0,) * a.ndim)
    specs = [whole(a) for a in pieces]
    if not first:
        last = edges[0].shape[1] // HOP - 1
        specs += [pl.BlockSpec((256, HOP), lambda i: (0, last)) for _ in edges]
    specs += [whole(table), whole(taper)]
    shape = jax.ShapeDtypeStruct((FR, 64, 1024), BF)
    return pl.pallas_call(
        functools.partial(stft_kernel, FR, first),
        grid=(1,),
        out_shape=[shape] * 8,
        in_specs=specs,
        out_specs=[pl.BlockSpec(shape.shape, lambda i: (0, 0, 0))] * 8,
        scratch_shapes=[pltpu.VMEM((512, WIN), BF)],
        cost_estimate=pl.CostEstimate(
            flops=2 * 512 * 512 * 1024 * FR, bytes_accessed=8 << 20, transcendentals=0
        ),
        name="stft",
    )(*pieces, *([] if first else edges), table, taper)


def local_stft_kernel(FR, begin, record, halo, table, taper, *refs):
    outs, ordered = refs[:8], refs[8]
    _, x, k = position()
    for i, (dx, dc) in enumerate(ROUTES):
        rows = table[route_to(x, k, dx, dc)].astype(F32)
        ordered[64 * i : 64 * (i + 1), :] = (rows * taper[...]).astype(BF)
    nt = (((1,), (1,)), ((), ()))
    hops = record.shape[1] // HOP
    for part in range(4):
        for f in range(FR):
            hop = SLICE * part + begin + f
            if hop + 1 < hops:
                got = lax.dot_general(
                    ordered[...],
                    record[:, HOP * hop : HOP * hop + WIN],
                    nt,
                    preferred_element_type=F32,
                )
            else:
                got = lax.dot_general(
                    ordered[:, :HOP], record[:, HOP * hop :], nt, preferred_element_type=F32
                ) + lax.dot_general(
                    ordered[:, HOP:], halo[...], nt, preferred_element_type=F32
                )
            got = got.astype(BF)
            for i in range(8):
                outs[i][part, f] = got[64 * i : 64 * (i + 1)]


def local_stft(FR, begin, record, halo, table, taper):
    whole = lambda a: pl.BlockSpec(a.shape, lambda i: (0,) * len(a.shape))
    shape = jax.ShapeDtypeStruct((4, FR, 64, 256), BF)
    return pl.pallas_call(
        functools.partial(local_stft_kernel, FR, begin),
        grid=(1,),
        out_shape=[shape] * 8,
        in_specs=[whole(a) for a in (record, halo, table, taper)],
        out_specs=[whole(shape)] * 8,
        scratch_shapes=[pltpu.VMEM((512, WIN), BF)],
        cost_estimate=pl.CostEstimate(
            flops=2 * 512 * 512 * 1024 * FR, bytes_accessed=8 << 20, transcendentals=0
        ),
        name="local_stft",
    )(record, halo, table, taper)


def repack_kernel(*refs):
    pieces, outs, (grid, sems) = refs[:8], refs[8:12], refs[12:]
    z, x, k = position()
    copies = [
        pltpu.make_async_copy(pieces[i], grid.at[route_from(x, k, dx, dc)], sems.at[i])
        for i, (dx, dc) in enumerate(ROUTES)
    ]
    for copy in copies:
        copy.start()
    for copy in copies:
        copy.wait()
    copies = [
        pltpu.make_async_copy(grid.at[:, lax.rem(z + s, 4)], outs[s], sems.at[s])
        for s in range(4)
    ]
    for copy in copies:
        copy.start()
    for copy in copies:
        copy.wait()


def repack(pieces):
    _, frames, rows, lanes = pieces[0].shape
    anywhere = pl.BlockSpec(memory_space=pl.ANY)
    return pl.pallas_call(
        repack_kernel,
        out_shape=[jax.ShapeDtypeStruct((8, frames, rows, lanes), BF)] * 4,
        in_specs=[anywhere] * 8,
        out_specs=[anywhere] * 4,
        scratch_shapes=[
            pltpu.VMEM((8, 4, frames, rows, lanes), BF),
            pltpu.SemaphoreType.DMA((8,)),
        ],
        cost_estimate=pl.CostEstimate(flops=1 << 20, bytes_accessed=4 << 20, transcendentals=0),
        name="repack",
    )(*pieces)


def plane_kernel(FR, x_first, *refs):
    count = 4 if x_first else 8
    pieces, masks, refs = refs[:count], refs[count : count + 5], refs[count + 5 :]
    dft, cosine, sine = refs[:3]
    outs, refs = refs[3:11], refs[11:]
    if x_first:
        grid, mixed, gate, sems, source = refs
    else:
        grid, mixed, gate, sems = refs
    rows = FR * 64
    BATCH = 16 // FR
    z, x, k = position()
    y = lax.div(lax.axis_index("tm"), 2)
    gates = [pltpu.make_async_copy(masks[0], gate.at[z], sems.at[8 * FR])]
    for j in range(4):
        low = pl.ds(pl.multiple_of(lax.rem(y + 4 - j, 4) * 8, 8), 8)
        for s in (1, 2, 3):
            gates.append(
                pltpu.make_async_copy(
                    masks[1 + j].at[s - 1],
                    gate.at[lax.rem(z + 4 - s, 4), low],
                    sems.at[8 * FR + 3 * j + s],
                )
            )
    if x_first:
        copies = [
            [
                pltpu.make_async_copy(
                    pieces[i].at[:, f], source.at[lax.rem(z + 4 - i, 4), :, f], sems.at[8 * f + i]
                )
                for i in range(4)
            ]
            for f in range(FR)
        ]
    else:
        copies = [
            [
                pltpu.make_async_copy(
                    pieces[i].at[f], grid.at[route_from(x, k, dx, dc), f], sems.at[8 * f + i]
                )
                for i, (dx, dc) in enumerate(ROUTES)
            ]
            for f in range(FR)
        ]
    for copy in sum(copies, []) + gates:
        copy.start()

    def forward(step, _):
        f = lax.div(step, 8)
        part = lax.rem(lax.div(step, 2), 4)
        lanes = pl.multiple_of(lax.rem(step, 2) * 128, 128)
        row = pl.ds(pl.multiple_of(part * 16, 16), 16)
        cut = pl.ds(pl.multiple_of(f * 64 + part * 16, 16), 16)

        def get(zz, w):
            if x_first:
                return split_tile(source[zz, w, f, row, pl.ds(lanes, 128)])
            return split_tile(grid[w, f, row, pl.ds(zz * 256 + lanes, 128)])

        for low in range(2):
            one, two = [], []
            for w in range(8):
                v = [get(zz, w) for zz in range(4)]
                if low == 0:
                    p, q = cadd(v[0], v[2]), cadd(v[1], v[3])
                else:
                    p, q = csub(v[0], v[2]), cturn(csub(v[1], v[3]), -1)
                one.append(cphase(cadd(p, q), w * low, 32, -1))
                two.append(cphase(csub(p, q), w * (low + 2), 32, -1))
            for j4, line in ((low, one), (low + 2, two)):
                for j8, (re, im) in enumerate(dft8(line, -1)):
                    m0 = j4 + 4 * j8
                    c = cosine[m0 : m0 + 1, pl.ds(lanes, 128)]
                    s = sine[m0 : m0 + 1, pl.ds(lanes, 128)]
                    mixed[m0, cut, pl.ds(lanes, 128)] = join_tile((re * c + im * s, im * c - re * s))
        return 0

    for f in range(FR):
        for copy in copies[f]:
            copy.wait()
        lax.fori_loop(8 * f, 8 * f + 8, forward, 0)
    for copy in gates:
        copy.wait()

    def filter_rows(step, _):
        at = pl.multiple_of(step * BATCH, BATCH)
        stack = mixed[pl.ds(at, BATCH)].reshape(BATCH * rows, 256)
        spread = jnp.dot(stack, dft[...], preferred_element_type=F32)
        spread = spread.reshape(BATCH, FR, 4, 2, 8, 512)
        re = spread[:, :, :, 0, :, :256] - spread[:, :, :, 1, :, 256:]
        im = spread[:, :, :, 0, :, 256:] + spread[:, :, :, 1, :, :256]
        keep = jnp.stack([gate[:, at + i].astype(F32) for i in range(BATCH)])[:, None]
        stack = jnp.stack([re * keep, im * keep], axis=3).reshape(BATCH * rows, 256).astype(BF)
        spread = jnp.dot(stack, dft[...], preferred_element_type=F32)
        spread = spread.reshape(BATCH, FR * 4, 2, 8, 512)
        for i in range(BATCH):
            re = spread[i, :, 0, :, :256] + spread[i, :, 1, :, 256:]
            im = spread[i, :, 1, :, :256] - spread[i, :, 0, :, 256:]
            c = cosine[pl.ds(at + i, 1), :]
            s = sine[pl.ds(at + i, 1), :]
            mixed[at + i] = (
                jnp.stack([re * c - im * s, re * s + im * c], axis=1).reshape(rows, 256).astype(BF)
            )
        return 0

    lax.fori_loop(0, 32 // BATCH, filter_rows, 0)

    def backward(step, _):
        f = lax.div(step, 8)
        part = lax.rem(lax.div(step, 2), 4)
        lanes = pl.multiple_of(lax.rem(step, 2) * 128, 128)
        row = pl.ds(pl.multiple_of(part * 16, 16), 16)
        cut = pl.ds(pl.multiple_of(f * 64 + part * 16, 16), 16)
        for odd in range(2):
            lines = []
            for j4 in range(4):
                v = [split_tile(mixed[j4 + 4 * j8, cut, pl.ds(lanes, 128)]) for j8 in range(8)]
                if odd == 0:
                    u = [cadd(v[i], v[i + 4]) for i in range(4)]
                else:
                    u = [cphase(csub(v[i], v[i + 4]), i, 8, 1) for i in range(4)]
                lines.append(
                    [cphase(a, (2 * i + odd) * j4, 32, 1) for i, a in enumerate(dft4(u, 1))]
                )
            for i in range(4):
                for zz, pair in enumerate(dft4([lines[j4][i] for j4 in range(4)], 1)):
                    grid[2 * i + odd, f, row, pl.ds(zz * 256 + lanes, 128)] = join_tile(pair)
        return 0

    copies = []
    for f in range(FR):
        lax.fori_loop(8 * f, 8 * f + 8, backward, 0)
        for i, (dx, dc) in enumerate(ROUTES):
            copies.append(
                pltpu.make_async_copy(
                    grid.at[route_to(x, k, dx, dc), f], outs[i].at[f], sems.at[8 * f + i]
                )
            )
            copies[-1].start()
    for copy in copies:
        copy.wait()


def plane(FR, x_first, pieces, masks, dft, cosine, sine):
    whole = lambda a: pl.BlockSpec(a.shape, lambda: (0,) * a.ndim)
    anywhere = pl.BlockSpec(memory_space=pl.ANY)
    shape = jax.ShapeDtypeStruct((FR, 64, 1024), BF)
    return pl.pallas_call(
        functools.partial(plane_kernel, FR, x_first),
        out_shape=[shape] * 8,
        in_specs=[anywhere] * (len(pieces) + 5) + [whole(a) for a in (dft, cosine, sine)],
        out_specs=[anywhere] * 8,
        scratch_shapes=[
            pltpu.VMEM((8, FR, 64, 1024), BF),
            pltpu.VMEM((32, FR * 64, 256), BF),
            pltpu.VMEM((4, 32, 8, 256), BF),
            pltpu.SemaphoreType.DMA((8 * FR + 13,)),
        ]
        + ([pltpu.VMEM((4, 8, FR, 64, 256), BF)] if x_first else []),
        cost_estimate=pl.CostEstimate(
            flops=4 * 32 * FR * 64 * 256 * 512 * 2, bytes_accessed=16 << 20, transcendentals=0
        ),
        name="plane",
    )(*pieces, *masks, dft, cosine, sine)


def istft_kernel(FR, first, last, *refs):
    pieces, refs = refs[:8], refs[8:]
    table, refs = refs[0], refs[1:]
    if not first:
        carried, refs = refs[0], refs[1:]
    outs, refs = refs[:4], refs[4:]
    if last:
        ends, refs = refs[:4], refs[4:]
    else:
        carry, refs = refs[0], refs[1:]
    grid, sems = refs
    z, x, k = position()
    copies = [
        pltpu.make_async_copy(pieces[i], grid.at[:, route_from(x, k, dx, dc)], sems.at[i])
        for i, (dx, dc) in enumerate(ROUTES)
    ]
    for copy in copies:
        copy.start()
    for copy in copies:
        copy.wait()
    tn = (((0,), (0,)), ((), ()))
    for s in range(4):
        place = pl.ds(pl.multiple_of(lax.rem(z + s, 4) * 256, 256), 256)
        tail = None if first else carried[s]
        for f in range(FR):
            bins = grid[f, :, :, place].reshape(512, 256)
            signal = lax.dot_general(bins, table[...].reshape(512, WIN), tn, preferred_element_type=F32)
            head = signal[:, :HOP]
            if tail is not None:
                head = head + tail
            outs[s][:, HOP * f : HOP * (f + 1)] = head.astype(BF)
            tail = signal[:, HOP:]
        if last:
            ends[s][...] = tail.astype(BF)
        else:
            carry[s] = tail


def istft(FR, pieces, table, carried, last):
    first = carried is None
    whole = lambda a: pl.BlockSpec(a.shape, lambda: (0,) * len(a.shape))
    anywhere = pl.BlockSpec(memory_space=pl.ANY)
    operands = [*pieces, table] + ([] if first else [carried])
    shapes = [jax.ShapeDtypeStruct((256, HOP * FR), BF)] * 4
    if last:
        shapes += [jax.ShapeDtypeStruct((256, HOP), BF)] * 4
    else:
        shapes.append(jax.ShapeDtypeStruct((4, 256, HOP), F32))
    return pl.pallas_call(
        functools.partial(istft_kernel, FR, first, last),
        out_shape=shapes,
        in_specs=[anywhere] * 8 + [whole(a) for a in operands[8:]],
        out_specs=[whole(a) for a in shapes],
        scratch_shapes=[pltpu.VMEM((FR, 8, 64, 1024), BF), pltpu.SemaphoreType.DMA((8,))],
        cost_estimate=pl.CostEstimate(
            flops=2 * 512 * 512 * 1024 * FR, bytes_accessed=8 << 20, transcendentals=0
        ),
        name="istft",
    )(*operands)


def join_kernel(*refs):
    count = 4 * len(CHUNKS)
    pieces, ends, out = refs[:count], refs[count : count + 4], refs[-1]
    z, _, _ = position()
    for s in range(4):
        source = lax.rem(z + 4 - s, 4)
        start = pl.multiple_of(source * (SLICE * HOP), SLICE * HOP)
        ahead = ends[(s + 1) % 4][...].astype(F32)
        for i, (begin, FR) in enumerate(zip(STARTS, CHUNKS)):
            block = pieces[4 * i + s][...].astype(F32)
            if i == 0:
                out[:, pl.ds(start, HOP)] = block[:, :HOP] + ahead
                if FR > 1:
                    out[:, pl.ds(start + HOP, HOP * (FR - 1))] = block[:, HOP:]
            else:
                out[:, pl.ds(start + HOP * begin, HOP * FR)] = block


def join(chunks, ends, span):
    pieces = [a for chunk in chunks for a in chunk] + ends
    rows = 32
    return pl.pallas_call(
        join_kernel,
        grid=(256 // rows,),
        out_shape=jax.ShapeDtypeStruct((256, span), F32),
        in_specs=[pl.BlockSpec((rows, a.shape[1]), lambda i: (i, 0)) for a in pieces],
        out_specs=pl.BlockSpec((rows, span), lambda i: (i, 0)),
        cost_estimate=pl.CostEstimate(flops=1 << 20, bytes_accessed=8 << 20, transcendentals=0),
        name="join",
    )(*pieces)


def steps(record, fan_mask):
    channels, span = record.shape
    wave, taper, dft, cosine, sine = (jnp.asarray(a) for a in make_tables())
    z, _, _ = position()

    def exchange(source, begin, count):
        size = (channels, HOP * count)
        out = {}
        for s in (*SHIFTS, 0):
            at = lax.rem(z + s, 4) * (SLICE * HOP) + begin * HOP
            part = lax.dynamic_slice(source, (0, at), size)
            out[s] = part if s == 0 else z_permute(part, s)
        return [out[s] for s in range(4)]

    halo = halo_permute(record[:, :HOP])
    raw = exchange(record, 0, CHUNKS[0] + 1)
    spectra = local_stft(CHUNKS[1], STARTS[1], record, halo, wave, taper)
    got = [spectra[0]] + [x_permute(spectra[j], j) for j in range(1, 8)]
    bins = 8 * lax.axis_index("chan") + jnp.arange(8)[:, None]
    weight = jnp.where(bins == 0, 1.0, 2.0).astype(F32) / (WIN * NCH)
    own_mask = (fan_mask.astype(F32) * weight).astype(BF).reshape(8, 256, 32).transpose(2, 0, 1)
    packed = repack(got)
    packed, _ = lax.optimization_barrier((packed, [raw[j] for j in HOLD]))
    second = [packed[0]] + [z_permute(packed[s], s) for s in (1, 2, 3)]
    masks = gather_masks(own_mask)

    spectra = stft(CHUNKS[0], raw, None, wave, taper)
    first = [spectra[0]] + [x_permute(spectra[j], j) for j in range(1, 8)]

    sums, carried = [], None
    for i, frames in enumerate(CHUNKS):
        back = plane(frames, i == 1, (first, second)[i], masks, dft, cosine, sine)
        got = [back[0]] + [x_permute(back[j], j) for j in range(1, 8)]
        last = i == len(CHUNKS) - 1
        result = istft(frames, got, wave, carried, last)
        sums.append([result[0]] + [z_permute(result[s], s) for s in (1, 2, 3)])
        carried = result[4]
    ends = [end_permute(result[4 + s], s) for s in range(4)]
    return join(sums, ends, span)


def solution(mesh):
    placed = (P("chan", "tm"), P("chan", None))
    return jax.shard_map(
        steps, mesh=mesh, in_specs=placed, out_specs=P("chan", "tm"), check_vma=False
    )
```
